512 devices in a mesh: grid: 256 (over x, y_lo, z, core), layer: 2 (over y_hi).
Axes of the slice: x: 4, y: 8 (y_hi: 2, y_lo: 4; y = y_hi * 4 + y_lo), z: 8, core: 2. Of those that a mesh axis runs over, the one named last changes fastest.
Arguments:
- x_tiles: bfloat16 [256, 512, 512], P('grid'), may hold values from -1.03 to 1.03, as said below
- pattern: int32 [256, 8, 8], P('grid'), may hold values from 0 to 1, as said below
Outputs:
- signed: bfloat16 [256, 128, 512], P('grid', 'layer')
The draws below stay inside these ranges and needn't reach their ends.
Inputs may be any that keep to these rules, and one draw needn't show every extreme that they name: `x_tiles`: tile (j, i) is the transpose of tile (i, j). symmetric: the block pattern of the whole matrix is its own transpose, and every diagonal block is kept.
All inputs are finite; a program needn't handle non-finite values.
Results may differ from the reference program's by a relative error of at most 0.013.
Values may be sent and summed in bfloat16 or wider, within the bound.
No kernel may reach another device: no remote copies, remote signals or barrier semaphores. Data moves between devices by JAX's collectives and lax.ppermute only.
A program may use at most 64 MiB of HBM per device.

```python
import math
import jax
import jax.numpy as jnp

BLOCK = 64
TILE_BLK = 8
SIDE = 16
TILE = 512
SLAB = 128
N_GRID = 256


def draw_x_tiles(key, part):
    order = SIDE * TILE
    first, second, third = jax.random.split(key, 3)
    spread = 0.6 / math.sqrt(64.0 * 13.0)
    noise = jnp.clip(jax.random.normal(first, (order, order), jnp.float32), -4.0, 4.0) * spread
    mirrored = (noise + noise.T) * 0.7071
    magnitude = jax.random.uniform(second, (order,), jnp.float32, 0.4, 0.9)
    signs = jnp.where(jax.random.bernoulli(third, 0.5, (order,)), 1.0, -1.0)
    whole = mirrored + jnp.diag(magnitude * signs)
    whole = whole.reshape(SIDE, TILE, SIDE, TILE).transpose(0, 2, 1, 3)
    return whole.reshape(SIDE * SIDE, TILE, TILE).astype(jnp.bfloat16)


def draw_pattern(key, part):
    count = SIDE * TILE_BLK
    first, second, third = jax.random.split(key, 3)
    reach = jax.random.randint(first, (count,), 1, 9)
    places = jnp.arange(count)
    apart = jnp.abs(places[:, None] - places[None, :])
    apart = jnp.minimum(apart, count - apart)
    inside = apart <= jnp.maximum(reach[:, None], reach[None, :])
    extra = jax.random.randint(second, (count, count), 0, 512)
    extra = jnp.where(places[:, None] <= places[None, :], extra, extra.T)
    whole = jnp.where(inside | (extra == 0), 1, 0).astype(jnp.int32)
    shuffle = jax.random.permutation(third, count).astype(jnp.int32)
    whole = jnp.take(jnp.take(whole, shuffle, axis=0), shuffle, axis=1)
    whole = whole.reshape(SIDE, TILE_BLK, SIDE, TILE_BLK).transpose(0, 2, 1, 3)
    return whole.reshape(SIDE * SIDE, TILE_BLK, TILE_BLK)


def setup_inputs(seed: int = 0) -> dict:
    seeds = jax.random.split(jax.random.key(seed), 3)
    return {
        "x_tiles": draw_x_tiles(jax.random.fold_in(seeds[2], 71), 0),
        "pattern": draw_pattern(jax.random.fold_in(seeds[2], 71), 0),
    }


def reference(x_tiles, pattern):
    order = SIDE * TILE
    mask = jnp.broadcast_to(pattern[:, :, None, :, None], (N_GRID, TILE_BLK, BLOCK, TILE_BLK, BLOCK))
    mask = mask.reshape(N_GRID, TILE, TILE).astype(jnp.bfloat16)
    tiles = x_tiles * mask
    matrix = tiles.reshape(SIDE, SIDE, TILE, TILE).transpose(0, 2, 1, 3).reshape(order, order)
    slab = matrix.reshape(SIDE, TILE, order)[:, :SLAB, :].reshape(SIDE * SLAB, order)
    squared = jnp.dot(slab, matrix, preferred_element_type=jnp.float32).astype(jnp.bfloat16)
    cubed = jnp.dot(squared, matrix, preferred_element_type=jnp.float32)
    signed = (1.5 * slab.astype(jnp.float32) - 0.5 * cubed).astype(jnp.bfloat16)
    return signed.reshape(SIDE, SLAB, SIDE, TILE).transpose(0, 2, 1, 3).reshape(N_GRID, SLAB, TILE)
```

```python
import jax
import jax.numpy as jnp
from jax import lax
from jax.sharding import Mesh, PartitionSpec as P

SIZES = {"x": 4, "y": 4, "z": 8, "c": 2, "l": 2}


def exchange(blocks, axis):
    return lax.all_to_all(blocks, axis, 0, 0, tiled=True)


def gather(block, axis):
    count = lax.axis_size(axis)
    return exchange(jnp.broadcast_to(block[None], (count,) + block.shape), axis)


def scatter_sum(blocks, axis):
    return jnp.sum(exchange(blocks, axis).astype(jnp.float32), axis=0)


def shards(x_tiles, pattern):
    half = jnp.bfloat16
    width = x_tiles.shape[1]
    slab = width // 4
    share = slab // 4
    blocks = pattern.shape[1]
    span = width // blocks
    nx, ny, nz = (lax.axis_size(a) for a in "xyz")
    core = lax.axis_index("c")
    layer = lax.axis_index("l")
    mask = jnp.broadcast_to(pattern[0][:, None, :, None], (blocks, span, blocks, span))
    tile = x_tiles[0] * mask.reshape(width, width).astype(half)
    other = lax.ppermute(tile, "c", [(0, 1), (1, 0)])
    pair = jnp.concatenate(
        [jnp.where(core == 0, tile, other), jnp.where(core == 0, other, tile)], axis=1
    )
    own = lax.dynamic_slice_in_dim(pair, (layer * 2 + core) * share, share, 0)
    rows = gather(gather(own, "y"), "x").reshape(nx * ny * share, 2 * width)
    partial = lax.dot_general(
        rows, pair, (((1,), (1,)), ((), ())), preferred_element_type=jnp.float32
    ).astype(half)
    squared = scatter_sum(partial.reshape(nz, -1, width), "z").astype(half)
    squared = gather(squared, "z").reshape(nx * ny * share, width)
    partial = jnp.dot(squared, pair, preferred_element_type=jnp.float32).astype(half)
    partial = scatter_sum(partial.reshape(nx, ny * share, 2 * width), "x").astype(half)
    cubed = scatter_sum(partial.reshape(ny, share, 2 * width), "y")
    signed = (1.5 * own.astype(jnp.float32) - 0.5 * cubed).astype(half)
    mine = jnp.where(core == 0, signed[:, :width], signed[:, width:])
    theirs = jnp.where(core == 0, signed[:, width:], signed[:, :width])
    back = lax.ppermute(theirs, "c", [(0, 1), (1, 0)])
    out = jnp.concatenate(
        [jnp.where(core == 0, mine, back), jnp.where(core == 0, back, mine)], axis=0
    )
    return out[None]


def solution(mesh, sizes=SIZES):
    fine = Mesh(mesh.devices.reshape(tuple(sizes.values())), tuple(sizes))
    grid = ("x", "y", "z", "c")
    specs = (P(grid, None, None), P(grid, None, None))
    return jax.shard_map(
        shards, mesh=fine, in_specs=specs, out_specs=P(grid, "l", None), check_vma=False
    )
```

```python
import jax
import jax.numpy as jnp
from jax import lax
from jax.sharding import Mesh, PartitionSpec as P


SIZES = {"x": 4, "h": 2, "p": 2, "z": 8, "c": 2, "l": 2}
NEAR = ("h", "p", "c")
SWAP = ((0, 1), (1, 0))


def exchange(blocks, axis):
    return lax.all_to_all(blocks, axis, 0, 0, tiled=True)


def gather(block, axis):
    count = lax.axis_size(axis)
    return exchange(jnp.broadcast_to(block[None], (count,) + block.shape), axis)


def total(blocks):
    return jnp.sum(blocks.astype(jnp.float32), axis=0)


def masked(tile, pattern):
    width, blocks = tile.shape[0], pattern.shape[0]
    span = width // blocks
    mask = jnp.broadcast_to(pattern[:, None, :, None], (blocks, span, blocks, span))
    return tile * mask.reshape(width, width).astype(tile.dtype)


def step(x_tiles, pattern):
    half = jnp.bfloat16
    width = x_tiles.shape[1]
    share = width // 32
    nx, nz = lax.axis_size("x"), lax.axis_size("z")
    first = lax.axis_index("c") == 0
    tile = masked(x_tiles[0], pattern[0])
    below = lax.ppermute(tile, "p", SWAP)
    beside = lax.ppermute(tile, "c", SWAP)
    corner = lax.ppermute(below, "c", SWAP)
    own = lax.dynamic_slice_in_dim(tile, lax.axis_index("l") * 4 * share, 4 * share, 0)

    parts = jnp.broadcast_to(own.reshape(1, 4, share, width), (2, 4, share, width))
    parts = exchange(parts.reshape(8, share, width), NEAR).reshape(4, 2, share, width)
    left, right = parts[:, 0], parts[:, 1]
    rows = jnp.concatenate(
        [jnp.where(first, left, right), jnp.where(first, right, left)], axis=2
    )
    rows = gather(rows, "x").reshape(-1, 2 * width)

    block = jnp.concatenate(
        [
            jnp.concatenate([tile, beside], axis=1),
            jnp.concatenate([below, corner], axis=1),
        ],
        axis=0,
    )
    partial = lax.dot_general(
        rows, block, (((1,), (1,)), ((), ())), preferred_element_type=jnp.float32
    ).astype(half)
    squared = total(exchange(partial.reshape(nz, -1, 2 * width), "z")).astype(half)
    squared = gather(squared, "z").reshape(-1, 2 * width)
    partial = jnp.dot(squared, block, preferred_element_type=jnp.float32).astype(half)
    partial = total(exchange(partial.reshape(nx, -1, 2 * width), "x")).astype(half)
    partial = partial.reshape(4, share, 2 * width)
    left, right = partial[:, :, :width], partial[:, :, width:]
    parts = jnp.stack(
        [jnp.where(first, left, right), jnp.where(first, right, left)], axis=1
    )
    parts = exchange(parts.reshape(8, share, width), NEAR)
    cubed = total(parts.reshape(2, 4 * share, width))
    signed = 1.5 * own.astype(jnp.float32) - 0.5 * cubed
    return signed.astype(half)[None]


def solution(mesh, sizes=SIZES):
    fine = Mesh(mesh.devices.reshape(tuple(sizes.values())), tuple(sizes))
    grid = ("x", "h", "p", "z", "c")
    specs = (P(grid, None, None), P(grid, None, None))
    return jax.shard_map(
        step, mesh=fine, in_specs=specs, out_specs=P(grid, "l", None), check_vma=False
    )
```

```python
import jax
import jax.numpy as jnp
from jax import lax
from jax.sharding import Mesh, PartitionSpec as P


SIZES = {"x": 4, "h": 2, "p": 2, "z": 8, "c": 2, "l": 2}
NEAR = ("h", "p", "c")
SWAP = ((0, 1), (1, 0))


def exchange(blocks, axis):
    return lax.all_to_all(blocks, axis, 0, 0, tiled=True)


def gather(block, axis):
    count = lax.axis_size(axis)
    return exchange(jnp.broadcast_to(block[None], (count,) + block.shape), axis)


def total(blocks):
    return jnp.sum(blocks.astype(jnp.float32), axis=0)


def masked(tile, pattern):
    width, blocks = tile.shape[0], pattern.shape[0]
    span = width // blocks
    mask = jnp.broadcast_to(pattern[:, None, :, None], (blocks, span, blocks, span))
    return tile * mask.reshape(width, width).astype(tile.dtype)


def step(x_tiles, pattern):
    half = jnp.bfloat16
    width = x_tiles.shape[1]
    share = width // 32
    nx, nz = lax.axis_size("x"), lax.axis_size("z")
    first = lax.axis_index("c") == 0
    tile = masked(x_tiles[0], pattern[0])
    below = lax.ppermute(tile, "p", SWAP)
    beside = lax.ppermute(tile, "c", SWAP)
    corner = lax.ppermute(below, "c", SWAP)
    own = lax.dynamic_slice_in_dim(tile, lax.axis_index("l") * 4 * share, 4 * share, 0)

    parts = jnp.broadcast_to(own.reshape(1, 4, share, width), (2, 4, share, width))
    parts = exchange(parts.reshape(8, share, width), NEAR)
    parts = parts.reshape(4, 2, share, width)
    left, right = parts[:, 0], parts[:, 1]
    rows = jnp.concatenate(
        [jnp.where(first, left, right), jnp.where(first, right, left)], axis=2
    )
    rows = gather(rows, "x").reshape(-1, 2 * width)

    block = jnp.concatenate(
        [
            jnp.concatenate([tile, beside], axis=1),
            jnp.concatenate([below, corner], axis=1),
        ],
        axis=0,
    )
    partial = lax.dot_general(
        rows, block, (((1,), (1,)), ((), ())), preferred_element_type=jnp.float32
    ).astype(half)
    squared = total(exchange(partial.reshape(nz, -1, 2 * width), "z")).astype(half)
    squared = gather(squared, "z").reshape(-1, 2 * width)
    partial = jnp.dot(squared, block, preferred_element_type=jnp.float32).astype(half)
    partial = partial.reshape(4 * nx, share, 2 * width)
    left, right = partial[:, :, :width], partial[:, :, width:]
    parts = jnp.stack(
        [jnp.where(first, left, right), jnp.where(first, right, left)], axis=1
    )
    parts = exchange(parts.reshape(8 * nx, share, width), ("x",) + NEAR)
    cubed = total(parts.reshape(2 * nx, 4 * share, width))
    signed = 1.5 * own.astype(jnp.float32) - 0.5 * cubed
    return signed.astype(half)[None]


def solution(mesh, sizes=SIZES):
    fine = Mesh(mesh.devices.reshape(tuple(sizes.values())), tuple(sizes))
    grid = ("x", "h", "p", "z", "c")
    specs = (P(grid, None, None), P(grid, None, None))
    return jax.shard_map(
        step, mesh=fine, in_specs=specs, out_specs=P(grid, "l", None), check_vma=False
    )
```

```python
import jax
import jax.numpy as jnp
from jax import lax
from jax.sharding import Mesh, PartitionSpec as P


SIZES = {"x": 4, "h": 2, "p": 2, "w": 4, "q": 2, "c": 2, "l": 2}
NEAR = ("h", "p", "q", "c")


def exchange(blocks, axis):
    return lax.all_to_all(blocks, axis, 0, 0, tiled=True)


def gather(block, axis):
    count = lax.axis_size(axis)
    return exchange(jnp.broadcast_to(block[None], (count,) + block.shape), axis)


def swap(tile, axis):
    return lax.ppermute(tile, axis, ((0, 1), (1, 0)))


def total(blocks):
    return jnp.sum(blocks.astype(jnp.float32), axis=0)


def masked(tile, pattern):
    width, blocks = tile.shape[0], pattern.shape[0]
    span = width // blocks
    mask = jnp.broadcast_to(pattern[:, None, :, None], (blocks, span, blocks, span))
    return tile * mask.reshape(width, width).astype(tile.dtype)


def turned(parts):
    q = lax.axis_index("q") == 0
    c = lax.axis_index("c") == 0
    a, b = jnp.where(q, parts[0], parts[2]), jnp.where(q, parts[1], parts[3])
    d, e = jnp.where(q, parts[2], parts[0]), jnp.where(q, parts[3], parts[1])
    return jnp.where(c, a, b), jnp.where(c, b, a), jnp.where(c, d, e), jnp.where(c, e, d)


def step(x_tiles, pattern):
    half = jnp.bfloat16
    width = x_tiles.shape[1]
    share = width // 64
    nx, nw = lax.axis_size("x"), lax.axis_size("w")
    upper = lax.axis_index("p") == 0
    tile = masked(x_tiles[0], pattern[0])
    own = lax.dynamic_slice_in_dim(tile, lax.axis_index("l") * 8 * share, 8 * share, 0)

    parts = own.reshape(2, 4, share, width).transpose(1, 0, 2, 3)
    parts = jnp.broadcast_to(parts.reshape(1, 4, 2 * share, width), (4, 4, 2 * share, width))
    parts = exchange(parts.reshape(16, 2 * share, width), NEAR)
    parts = parts.reshape(4, 4, 2 * share, width)
    rows = jnp.concatenate(turned([parts[:, k] for k in range(4)]), axis=2)
    rows = gather(rows, "x").reshape(-1, 4 * width)

    along = swap(tile, "q")
    tiles = [tile, swap(tile, "c"), along, swap(along, "c")]
    below = swap(tile, "p")
    corner = swap(along, "p")
    lower = [below, swap(below, "c"), corner, swap(corner, "c")]

    block = jnp.concatenate(tiles, axis=1)
    partial = lax.dot_general(
        rows, block, (((1,), (1,)), ((), ())), preferred_element_type=jnp.float32
    ).astype(half)
    squared = total(exchange(partial.reshape(nw, -1, width), "w")).astype(half)
    squared = squared.reshape(4, 2, share, width).transpose(1, 0, 2, 3)
    squared = jnp.broadcast_to(
        squared.reshape(2, 1, 4 * share, width), (2, nw, 4 * share, width)
    )
    squared = exchange(squared.reshape(2 * nw, 4 * share, width), ("p", "w"))
    squared = squared.reshape(2, nw * 4 * share, width)
    squared = jnp.concatenate(
        [
            jnp.where(upper, squared[0], squared[1]),
            jnp.where(upper, squared[1], squared[0]),
        ],
        axis=1,
    )
    block = jnp.concatenate([block, jnp.concatenate(lower, axis=1)], axis=0)
    partial = jnp.dot(squared, block, preferred_element_type=jnp.float32).astype(half)
    partial = partial.reshape(4 * nx, share, 4 * width)
    parts = turned([partial[:, :, k * width : (k + 1) * width] for k in range(4)])
    parts = jnp.stack(parts, axis=1).reshape(16 * nx, share, width)
    parts = exchange(parts, ("x",) + NEAR)
    cubed = total(parts.reshape(2 * nx, 8 * share, width))
    signed = 1.5 * own.astype(jnp.float32) - 0.5 * cubed
    return signed.astype(half)[None]


def solution(mesh, sizes=SIZES):
    fine = Mesh(mesh.devices.reshape(tuple(sizes.values())), tuple(sizes))
    grid = ("x", "h", "p", "w", "q", "c")
    specs = (P(grid, None, None), P(grid, None, None))
    return jax.shard_map(
        step, mesh=fine, in_specs=specs, out_specs=P(grid, "l", None), check_vma=False
    )
```

```python
import jax
import jax.numpy as jnp
from jax import lax
from jax.experimental import pallas as pl
from jax.experimental.pallas import tpu as pltpu
from jax.sharding import Mesh, PartitionSpec as P


SIZES = {"x": 4, "h": 2, "p": 2, "w": 4, "q": 2, "c": 2, "l": 2}
VMEM = pl.BlockSpec(memory_space=pltpu.VMEM)


def exchange(blocks, axis):
    return lax.all_to_all(blocks, axis, 0, 0, tiled=True)


def spread(block, axis):
    count = lax.axis_size(axis)
    return exchange(jnp.broadcast_to(block[None], (count,) + block.shape), axis)


def swap(tile, axis):
    return lax.ppermute(tile, axis, ((0, 1), (1, 0)))


def total(blocks):
    return jnp.sum(blocks.astype(jnp.float32), axis=0)


def masked(tile, pattern):
    width, blocks = tile.shape[0], pattern.shape[0]
    span = width // blocks
    mask = jnp.broadcast_to(pattern[:, None, :, None], (blocks, span, blocks, span))
    return tile * mask.reshape(width, width).astype(tile.dtype)


def product_kernel(place_ref, left_ref, *refs):
    tiles, lower, out_ref = refs[:4], refs[4:8], refs[8]
    width = tiles[0].shape[0]
    share = out_ref.shape[2]
    left = left_ref[:, :width]
    right = left_ref[:, width:]
    place = place_ref[0]
    for k in range(4):
        part = jnp.dot(left, tiles[k][...], preferred_element_type=jnp.float32)
        part += jnp.dot(right, lower[k][...], preferred_element_type=jnp.float32)
        part = part.astype(out_ref.dtype).reshape(-1, share, width)
        out_ref[:, lax.bitwise_xor(place, k)] = part


def product(place, left, tiles, lower, share):
    rows, width = left.shape[0], tiles[0].shape[0]
    return pl.pallas_call(
        product_kernel,
        out_shape=jax.ShapeDtypeStruct((rows // share, 4, share, width), left.dtype),
        in_specs=[pl.BlockSpec(memory_space=pltpu.SMEM)] + [VMEM] * 9,
        out_specs=VMEM,
        compiler_params=pltpu.CompilerParams(vmem_limit_bytes=16 << 20),
        cost_estimate=pl.CostEstimate(
            flops=16 * rows * width * width,
            bytes_accessed=20 * width * width,
            transcendentals=0,
        ),
    )(place, left, *tiles, *lower)


def step(x_tiles, pattern):
    half = jnp.bfloat16
    width = x_tiles.shape[1]
    share = width // 64
    nx = lax.axis_size("x")
    first = lax.axis_index("c") == 0
    tile = masked(x_tiles[0], pattern[0])
    own = lax.dynamic_slice_in_dim(tile, lax.axis_index("l") * 8 * share, 8 * share, 0)

    parts = own.reshape(2, 2, 2, share, width).transpose(0, 2, 1, 3, 4)
    parts = jnp.broadcast_to(
        parts.reshape(1, 4, 2 * share, width), (2, 4, 2 * share, width)
    )
    parts = exchange(parts.reshape(8, 2 * share, width), ("h", "p", "c"))
    parts = parts.reshape(4, 2, 2, share, width)
    left, right = parts[:, 0], parts[:, 1]
    rows = jnp.concatenate(
        [jnp.where(first, left, right), jnp.where(first, right, left)], axis=3
    )
    rows = rows.transpose(1, 0, 2, 3).reshape(8 * share, 2 * width)
    rows = spread(rows, "x").reshape(-1, 2 * width)

    below = swap(tile, "p")
    along = swap(tile, "q")
    corner = swap(along, "p")
    beside = swap(tile, "c")
    below_beside = swap(below, "c")
    tiles = [tile, beside, along, swap(along, "c")]
    lower = [below, below_beside, corner, swap(corner, "c")]

    block = jnp.concatenate(
        [
            jnp.concatenate([tile, beside], axis=1),
            jnp.concatenate([below, below_beside], axis=1),
        ],
        axis=0,
    )
    partial = lax.dot_general(
        rows, block, (((1,), (1,)), ((), ())), preferred_element_type=jnp.float32
    ).astype(half)
    partial = partial.reshape(2 * lax.axis_size("w"), -1, 2 * width)
    squared = total(exchange(partial, ("w", "q"))).astype(half)
    squared = spread(squared, "w").reshape(-1, 2 * width)
    place = lax.axis_index("q") * 2 + lax.axis_index("c")
    parts = product(place.reshape(1), squared, tiles, lower, share)
    parts = parts.reshape(16 * nx, share, width)
    parts = exchange(parts, ("x", "h", "p", "q", "c"))
    cubed = total(parts.reshape(2 * nx, 8 * share, width))
    signed = 1.5 * own.astype(jnp.float32) - 0.5 * cubed
    return signed.astype(half)[None]


def solution(mesh, sizes=SIZES):
    fine = Mesh(mesh.devices.reshape(tuple(sizes.values())), tuple(sizes))
    grid = ("x", "h", "p", "w", "q", "c")
    specs = (P(grid, None, None), P(grid, None, None))
    return jax.shard_map(
        step, mesh=fine, in_specs=specs, out_specs=P(grid, "l", None), check_vma=False
    )
```

```python
import jax
import jax.numpy as jnp
from jax import lax
from jax.experimental import pallas as pl
from jax.experimental.pallas import tpu as pltpu
from jax.sharding import Mesh, PartitionSpec as P


SIZES = {"x": 4, "h": 2, "p": 2, "w": 4, "q": 2, "c": 2, "l": 2}
VMEM = pl.BlockSpec(memory_space=pltpu.VMEM)


def exchange(blocks, axis):
    return lax.all_to_all(blocks, axis, 0, 0, tiled=True)


def ring(block, axis):
    count = lax.axis_size(axis)
    got = {0: block}
    for far in sorted(range(1, count), key=lambda d: -min(d, count - d)):
        route = [(i, (i - far) % count) for i in range(count)]
        got[far] = lax.ppermute(block, axis, route)
    return [got[d] for d in range(count)]


def swap(tile, axis):
    return lax.ppermute(tile, axis, ((0, 1), (1, 0)))


def total(blocks):
    return jnp.sum(blocks.astype(jnp.float32), axis=0)


def mask_kernel(layer_ref, tile_ref, pattern_ref, out_ref, parts_ref):
    width = tile_ref.shape[1]
    blocks = pattern_ref.shape[1]
    span, share = width // blocks, width // 64
    number = lax.broadcasted_iota(jnp.int32, (blocks, width), 0)
    place = lax.broadcasted_iota(jnp.int32, (blocks, width), 1)
    inside = (place >= number * span) & (place < number * span + span)
    wide = jnp.dot(
        pattern_ref[0].astype(jnp.float32),
        inside.astype(jnp.float32),
        preferred_element_type=jnp.float32,
    )
    for k in range(blocks):
        rows = pl.ds(k * span, span)
        kept = tile_ref[0, rows, :].astype(jnp.float32) * wide[k : k + 1]
        out_ref[rows, :] = kept.astype(out_ref.dtype)
    first = layer_ref[0] * (8 * share)
    for k in range(8):
        p, q, c = k // 4, k // 2 % 2, k % 2
        start = pl.multiple_of(first + k * share, share)
        piece = out_ref[pl.ds(start, share), :]
        for h in range(2):
            parts_ref[4 * h + 2 * p + c, pl.ds(q * share, share), :] = piece


def masked(layer, tile, pattern):
    width = tile.shape[1]
    return pl.pallas_call(
        mask_kernel,
        out_shape=(
            jax.ShapeDtypeStruct((width, width), tile.dtype),
            jax.ShapeDtypeStruct((8, width // 32, width), tile.dtype),
        ),
        in_specs=[pl.BlockSpec(memory_space=pltpu.SMEM), VMEM, VMEM],
        out_specs=(VMEM, VMEM),
        compiler_params=pltpu.CompilerParams(vmem_limit_bytes=8 << 20),
        name="mask",
    )(layer, tile, pattern)


def first_kernel(*refs):
    count = len(refs) - 6
    chunks, tiles, out_ref, rows_ref = refs[:count], refs[count : count + 4], refs[-2], refs[-1]
    width = tiles[0].shape[0]
    height = chunks[0].shape[0]
    for k in range(count):
        rows_ref[pl.ds(k * height, height), :] = chunks[k][...]
    turned = (((1,), (1,)), ((), ()))
    left, right = rows_ref[:, :width], rows_ref[:, width:]
    for k in range(2):
        part = lax.dot_general(
            left, tiles[2 * k][...], turned, preferred_element_type=jnp.float32
        )
        part += lax.dot_general(
            right, tiles[2 * k + 1][...], turned, preferred_element_type=jnp.float32
        )
        out_ref[:, k * width : (k + 1) * width] = part.astype(out_ref.dtype)


def first_product(chunks, tiles):
    width = tiles[0].shape[0]
    shape = (len(chunks) * chunks[0].shape[0], 2 * width)
    return pl.pallas_call(
        first_kernel,
        out_shape=jax.ShapeDtypeStruct(shape, tiles[0].dtype),
        in_specs=[VMEM] * (len(chunks) + 4),
        out_specs=VMEM,
        scratch_shapes=[pltpu.VMEM(shape, tiles[0].dtype)],
        compiler_params=pltpu.CompilerParams(vmem_limit_bytes=16 << 20),
        name="first",
    )(*chunks, *tiles)


def second_kernel(place_ref, *refs):
    count = len(refs) - 10
    chunks, tiles, lower = refs[:count], refs[count : count + 4], refs[count + 4 : count + 8]
    out_ref, rows_ref = refs[-2], refs[-1]
    width = tiles[0].shape[0]
    height = chunks[0].shape[0]
    for k in range(count):
        rows_ref[pl.ds(k * height, height), :] = chunks[k][...]
    left, right = rows_ref[:, :width], rows_ref[:, width:]
    for k in range(4):
        part = jnp.dot(left, tiles[k][...], preferred_element_type=jnp.float32)
        part += jnp.dot(right, lower[k][...], preferred_element_type=jnp.float32)
        part = part.astype(out_ref.dtype)
        column = lax.bitwise_xor(place_ref[0], k)
        for e in range(count):
            piece = part[e * height : (e + 1) * height]
            piece = piece.reshape(out_ref.shape[1], out_ref.shape[3], width)
            out_ref[lax.rem(place_ref[1] + e, count), :, column] = piece


def second_product(place, chunks, tiles, lower, share):
    count, (height, width) = len(chunks), chunks[0].shape
    half = chunks[0].dtype
    return pl.pallas_call(
        second_kernel,
        out_shape=jax.ShapeDtypeStruct((count, height // share, 4, share, width // 2), half),
        in_specs=[pl.BlockSpec(memory_space=pltpu.SMEM)] + [VMEM] * (count + 8),
        out_specs=VMEM,
        scratch_shapes=[pltpu.VMEM((count * height, width), half)],
        compiler_params=pltpu.CompilerParams(vmem_limit_bytes=16 << 20),
        name="second",
    )(place, *chunks, *tiles, *lower)


def step(x_tiles, pattern):
    half = jnp.bfloat16
    width = x_tiles.shape[1]
    share = width // 64
    nx = lax.axis_size("x")
    first = lax.axis_index("c") == 0
    layer = lax.axis_index("l")
    tile, parts = masked(layer.reshape(1), x_tiles, pattern)
    own = lax.dynamic_slice_in_dim(tile, layer * 8 * share, 8 * share, 0)
    parts = exchange(parts, ("h", "p", "c"))
    parts = parts.reshape(4, 2, 2, share, width)
    left, right = parts[:, 0], parts[:, 1]
    rows = jnp.concatenate(
        [jnp.where(first, left, right), jnp.where(first, right, left)], axis=3
    )
    rows = rows.transpose(1, 0, 2, 3).reshape(8 * share, 2 * width)
    rows = ring(rows, "x")

    below = swap(tile, "p")
    along = swap(tile, "q")
    corner = swap(along, "p")
    beside = swap(tile, "c")
    below_beside = swap(below, "c")
    tiles = [tile, beside, along, swap(along, "c")]
    lower = [below, below_beside, corner, swap(corner, "c")]

    partial = first_product(rows, [tile, beside, below, below_beside])
    partial = partial.reshape(2 * nx, -1, 2 * width)
    squared = total(exchange(partial, ("w", "q"))).astype(half)
    squared = ring(squared, "w")
    turn = lax.rem(lax.axis_index("x") + lax.axis_index("w"), nx)
    place = jnp.stack([lax.axis_index("q") * 2 + lax.axis_index("c"), turn])
    parts = second_product(place.astype(jnp.int32), squared, tiles, lower, share)
    parts = parts.reshape(16 * nx, share, width)
    parts = exchange(parts, ("x", "h", "p", "q", "c"))
    cubed = total(parts.reshape(2 * nx, 8 * share, width))
    signed = 1.5 * own.astype(jnp.float32) - 0.5 * cubed
    return signed.astype(half)[None]


def solution(mesh, sizes=SIZES):
    fine = Mesh(mesh.devices.reshape(tuple(sizes.values())), tuple(sizes))
    grid = ("x", "h", "p", "w", "q", "c")
    specs = (P(grid, None, None), P(grid, None, None))
    return jax.shard_map(
        step, mesh=fine, in_specs=specs, out_specs=P(grid, "l", None), check_vma=False
    )
```

```python
import jax
import jax.numpy as jnp
from jax import lax
from jax.experimental import pallas as pl
from jax.experimental.pallas import tpu as pltpu
from jax.sharding import Mesh, PartitionSpec as P


SIZES = {"x": 4, "h": 2, "p": 2, "z": 8, "c": 2, "l": 2}
SMEM = pl.BlockSpec(memory_space=pltpu.SMEM)
VMEM = pl.BlockSpec(memory_space=pltpu.VMEM)
ANY = pl.BlockSpec(memory_space=pl.ANY)


def call(kernel, shape, dtype, specs, flops=0):
    size = 2
    for extent in shape:
        size *= extent
    return pl.pallas_call(
        kernel,
        out_shape=jax.ShapeDtypeStruct(shape, dtype),
        in_specs=specs,
        out_specs=VMEM,
        compiler_params=pltpu.CompilerParams(vmem_limit_bytes=16 << 20),
        cost_estimate=pl.CostEstimate(
            flops=flops, bytes_accessed=2 * size, transcendentals=0
        ),
    )


def exchange(blocks, axis):
    return lax.all_to_all(blocks, axis, 0, 0, tiled=True)


def swap(tile, axis):
    return lax.ppermute(tile, axis, ((0, 1), (1, 0)))


def total(blocks):
    return jnp.sum(blocks.astype(jnp.float32), axis=0)


def masked(tile, pattern):
    width, blocks = tile.shape[0], pattern.shape[0]
    span = width // blocks
    mask = jnp.broadcast_to(pattern[:, None, :, None], (blocks, span, blocks, span))
    return tile * mask.reshape(width, width).astype(tile.dtype)


def send_kernel(layer_ref, tile_ref, pattern_ref, out_ref, own_ref, rows_ref, kept_ref, sems):
    share, width = out_ref.shape[1:]
    blocks = pattern_ref.shape[1]
    height = 4 * share
    span = width // blocks
    start = pl.multiple_of(layer_ref[0] * height, height)
    rows = pltpu.make_async_copy(tile_ref.at[0, pl.ds(start, height)], rows_ref, sems.at[0])
    kept = pltpu.make_async_copy(pattern_ref, kept_ref, sems.at[1])
    rows.start()
    kept.start()
    number = lax.broadcasted_iota(jnp.int32, (blocks, width), 0)
    place = lax.broadcasted_iota(jnp.int32, (blocks, width), 1)
    inside = (place >= number * span) & (place < number * span + span)
    kept.wait()
    wide = jnp.dot(
        kept_ref[0].astype(jnp.float32),
        inside.astype(jnp.float32),
        preferred_element_type=jnp.float32,
    )
    tall = lax.broadcasted_iota(jnp.int32, (height, blocks), 0) + start
    line = lax.broadcasted_iota(jnp.int32, (height, blocks), 1)
    chosen = (tall >= line * span) & (tall < line * span + span)
    mask = jnp.dot(chosen.astype(jnp.float32), wide, preferred_element_type=jnp.float32)
    rows.wait()
    piece = (rows_ref[...].astype(jnp.float32) * mask).astype(out_ref.dtype)
    own_ref[...] = piece
    for k in range(out_ref.shape[0]):
        part = k % 4 * share
        out_ref[k] = piece[part : part + share]


def rows_kernel(core_ref, parts_ref, out_ref):
    share, width = parts_ref.shape[1:]
    for k in range(parts_ref.shape[0] // 2):
        for side in range(2):
            piece = parts_ref[2 * k + lax.bitwise_xor(core_ref[0], side)]
            for far in range(out_ref.shape[0]):
                rows, columns = pl.ds(k * share, share), pl.ds(side * width, width)
                out_ref[far, rows, columns] = piece


def first_kernel(rows_ref, a_ref, b_ref, c_ref, d_ref, out_ref):
    width = a_ref.shape[0]
    turned = (((1,), (1,)), ((), ()))
    left, right = rows_ref[:, :width], rows_ref[:, width:]
    for k, (one, two) in enumerate(((a_ref, b_ref), (c_ref, d_ref))):
        part = lax.dot_general(left, one[...], turned, preferred_element_type=jnp.float32)
        part += lax.dot_general(right, two[...], turned, preferred_element_type=jnp.float32)
        out_ref[:, k] = part.astype(out_ref.dtype).reshape(out_ref.shape[0], -1, width)


def second_kernel(core_ref, left_ref, a_ref, b_ref, c_ref, d_ref, out_ref):
    width = a_ref.shape[0]
    left = left_ref[:, 0].reshape(-1, width)
    right = left_ref[:, 1].reshape(-1, width)
    for k, (one, two) in enumerate(((a_ref, c_ref), (b_ref, d_ref))):
        part = jnp.dot(left, one[...], preferred_element_type=jnp.float32)
        part += jnp.dot(right, two[...], preferred_element_type=jnp.float32)
        part = part.astype(out_ref.dtype).reshape(-1, out_ref.shape[2], width)
        out_ref[:, lax.bitwise_xor(core_ref[0], k)] = part


def step(x_tiles, pattern):
    half = jnp.bfloat16
    width = x_tiles.shape[1]
    share = width // 32
    nx, nz = lax.axis_size("x"), lax.axis_size("z")
    core = lax.axis_index("c").reshape(1)
    layer = lax.axis_index("l").reshape(1)
    height = 4 * nx * share
    flops = 8 * height * width * width

    parts, own = pl.pallas_call(
        send_kernel,
        out_shape=(
            jax.ShapeDtypeStruct((8, share, width), half),
            jax.ShapeDtypeStruct((4 * share, width), half),
        ),
        in_specs=[SMEM, ANY, ANY],
        out_specs=(VMEM, VMEM),
        scratch_shapes=(
            pltpu.VMEM((4 * share, width), half),
            pltpu.VMEM(pattern.shape, jnp.int32),
            pltpu.SemaphoreType.DMA((2,)),
        ),
        name="send",
    )(layer, x_tiles, pattern)
    parts = exchange(parts, ("h", "p", "c"))
    rows = call(rows_kernel, (nx, 4 * share, 2 * width), half, [SMEM, VMEM])
    rows = exchange(rows(core, parts), "x").reshape(height, 2 * width)

    tile = masked(x_tiles[0], pattern[0])
    below = swap(tile, "p")
    tiles = [tile, swap(tile, "c"), below, swap(below, "c")]

    shape = (nz, 2, height // nz, width)
    partial = call(first_kernel, shape, half, [VMEM] * 5, flops)(rows, *tiles)
    partial = partial.reshape(nz, -1, width)
    squared = total(exchange(partial, "z")).astype(half)
    squared = jnp.broadcast_to(squared[None], (nz,) + squared.shape)
    squared = exchange(squared, "z").reshape(shape)
    shape = (4 * nx, 2, share, width)
    parts = call(second_kernel, shape, half, [SMEM] + [VMEM] * 5, flops)
    parts = parts(core, squared, *tiles).reshape(8 * nx, share, width)
    parts = exchange(parts, ("x", "h", "p", "c"))
    cubed = total(parts.reshape(2 * nx, 4 * share, width))
    signed = 1.5 * own.astype(jnp.float32) - 0.5 * cubed
    return signed.astype(half)[None]


def solution(mesh, sizes=SIZES):
    fine = Mesh(mesh.devices.reshape(tuple(sizes.values())), tuple(sizes))
    grid = ("x", "h", "p", "z", "c")
    specs = (P(grid, None, None), P(grid, None, None))
    return jax.shard_map(
        step, mesh=fine, in_specs=specs, out_specs=P(grid, "l", None), check_vma=False
    )
```

```python
import jax
import jax.numpy as jnp
from jax import lax
from jax.experimental import pallas as pl
from jax.experimental.pallas import tpu as pltpu
from jax.sharding import Mesh, PartitionSpec as P


SIZES = {"x": 4, "h": 2, "p": 2, "w": 4, "q": 2, "c": 2, "l": 2}
SMEM = pl.BlockSpec(memory_space=pltpu.SMEM)
VMEM = pl.BlockSpec(memory_space=pltpu.VMEM)
ANY = pl.BlockSpec(memory_space=pl.ANY)


def call(kernel, shape, dtype, specs, flops=0):
    size = 2
    for extent in shape:
        size *= extent
    return pl.pallas_call(
        kernel,
        out_shape=jax.ShapeDtypeStruct(shape, dtype),
        in_specs=specs,
        out_specs=VMEM,
        compiler_params=pltpu.CompilerParams(vmem_limit_bytes=16 << 20),
        cost_estimate=pl.CostEstimate(
            flops=flops, bytes_accessed=2 * size, transcendentals=0
        ),
    )


def exchange(blocks, axis):
    return lax.all_to_all(blocks, axis, 0, 0, tiled=True)


def swap(tile, axis):
    return lax.ppermute(tile, axis, ((0, 1), (1, 0)))


def total(blocks):
    return jnp.sum(blocks.astype(jnp.float32), axis=0)


def masked(tile, pattern):
    width, blocks = tile.shape[0], pattern.shape[0]
    span = width // blocks
    mask = jnp.broadcast_to(pattern[:, None, :, None], (blocks, span, blocks, span))
    return tile * mask.reshape(width, width).astype(tile.dtype)


def send_kernel(layer_ref, tile_ref, pattern_ref, out_ref, own_ref, rows_ref, kept_ref, sems):
    share, width = out_ref.shape[1:]
    blocks = pattern_ref.shape[1]
    height = 4 * share
    small = share // 2
    span = width // blocks
    start = pl.multiple_of(layer_ref[0] * height, height)
    rows = pltpu.make_async_copy(tile_ref.at[0, pl.ds(start, height)], rows_ref, sems.at[0])
    kept = pltpu.make_async_copy(pattern_ref, kept_ref, sems.at[1])
    rows.start()
    kept.start()
    number = lax.broadcasted_iota(jnp.int32, (blocks, width), 0)
    place = lax.broadcasted_iota(jnp.int32, (blocks, width), 1)
    inside = (place >= number * span) & (place < number * span + span)
    kept.wait()
    wide = jnp.dot(
        kept_ref[0].astype(jnp.float32),
        inside.astype(jnp.float32),
        preferred_element_type=jnp.float32,
    )
    tall = lax.broadcasted_iota(jnp.int32, (height, blocks), 0) + start
    line = lax.broadcasted_iota(jnp.int32, (height, blocks), 1)
    chosen = (tall >= line * span) & (tall < line * span + span)
    mask = jnp.dot(chosen.astype(jnp.float32), wide, preferred_element_type=jnp.float32)
    rows.wait()
    piece = (rows_ref[...].astype(jnp.float32) * mask).astype(out_ref.dtype)
    own_ref[...] = piece
    for k in range(out_ref.shape[0]):
        p, c = k // 2 % 2, k % 2
        for q in range(2):
            part = (4 * p + 2 * q + c) * small
            out_ref[k, q * small : (q + 1) * small] = piece[part : part + small]


def rows_kernel(core_ref, parts_ref, out_ref):
    count, share, width = parts_ref.shape
    small = share // 2
    for k in range(count // 2):
        for side in range(2):
            columns = pl.ds(side * width, width)
            piece = parts_ref[2 * k + lax.bitwise_xor(core_ref[0], side)]
            for q in range(2):
                rows = pl.ds((q * (count // 2) + k) * small, small)
                for far in range(out_ref.shape[0]):
                    out_ref[far, rows, columns] = piece[q * small : (q + 1) * small]


def sum_kernel(parts_ref, out_ref):
    value = parts_ref[0].astype(jnp.float32)
    for k in range(1, parts_ref.shape[0]):
        value += parts_ref[k].astype(jnp.float32)
    for k in range(out_ref.shape[0]):
        out_ref[k] = value.astype(out_ref.dtype)


def first_kernel(rows_ref, a_ref, b_ref, c_ref, d_ref, out_ref):
    width = a_ref.shape[0]
    turned = (((1,), (1,)), ((), ()))
    left, right = rows_ref[:, :width], rows_ref[:, width:]
    for k, (one, two) in enumerate(((a_ref, b_ref), (c_ref, d_ref))):
        part = lax.dot_general(left, one[...], turned, preferred_element_type=jnp.float32)
        part += lax.dot_general(right, two[...], turned, preferred_element_type=jnp.float32)
        out_ref[:, k] = part.astype(out_ref.dtype).reshape(out_ref.shape[0], -1, width)


def second_kernel(place_ref, left_ref, *refs):
    tiles, lower, out_ref = refs[:4], refs[4:8], refs[8]
    width = tiles[0].shape[0]
    left = left_ref[:, 0].reshape(-1, width)
    right = left_ref[:, 1].reshape(-1, width)
    for k in range(4):
        part = jnp.dot(left, tiles[k][...], preferred_element_type=jnp.float32)
        part += jnp.dot(right, lower[k][...], preferred_element_type=jnp.float32)
        part = part.astype(out_ref.dtype).reshape(-1, out_ref.shape[2], width)
        out_ref[:, lax.bitwise_xor(place_ref[0], k)] = part


def step(x_tiles, pattern):
    half = jnp.bfloat16
    width = x_tiles.shape[1]
    share = width // 32
    nx, nw = lax.axis_size("x"), lax.axis_size("w")
    core = lax.axis_index("c").reshape(1)
    layer = lax.axis_index("l").reshape(1)
    height = 4 * nx * share
    flops = 8 * height * width * width

    parts, own = pl.pallas_call(
        send_kernel,
        out_shape=(
            jax.ShapeDtypeStruct((8, share, width), half),
            jax.ShapeDtypeStruct((4 * share, width), half),
        ),
        in_specs=[SMEM, ANY, ANY],
        out_specs=(VMEM, VMEM),
        scratch_shapes=(
            pltpu.VMEM((4 * share, width), half),
            pltpu.VMEM(pattern.shape, jnp.int32),
            pltpu.SemaphoreType.DMA((2,)),
        ),
        name="send",
    )(layer, x_tiles, pattern)
    parts = exchange(parts, ("h", "p", "c"))
    rows = call(rows_kernel, (nx, 4 * share, 2 * width), half, [SMEM, VMEM])
    rows = exchange(rows(core, parts), "x").reshape(height, 2 * width)

    tile = masked(x_tiles[0], pattern[0])
    below = swap(tile, "p")
    along = swap(tile, "q")
    corner = swap(along, "p")
    tiles = [tile, swap(tile, "c"), along, swap(along, "c")]
    lower = [below, swap(below, "c"), corner, swap(corner, "c")]

    shape = (2 * nw, 2, height // (2 * nw), width)
    partial = call(first_kernel, shape, half, [VMEM] * 5, flops)
    partial = partial(rows, tiles[0], tiles[1], lower[0], lower[1])
    partial = exchange(partial.reshape(2 * nw, -1, width), ("w", "q"))
    squared = call(sum_kernel, (nw,) + partial.shape[1:], half, [VMEM])(partial)
    squared = exchange(squared, "w").reshape((nw,) + shape[1:])
    place = 2 * lax.axis_index("q") + lax.axis_index("c")
    shape = (4 * nx, 4, share // 2, width)
    parts = call(second_kernel, shape, half, [SMEM] + [VMEM] * 9, flops)
    parts = parts(place.reshape(1), squared, *tiles, *lower)
    parts = parts.reshape(16 * nx, share // 2, width)
    parts = exchange(parts, ("x", "h", "p", "q", "c"))
    cubed = total(parts.reshape(2 * nx, 4 * share, width))
    signed = 1.5 * own.astype(jnp.float32) - 0.5 * cubed
    return signed.astype(half)[None]


def solution(mesh, sizes=SIZES):
    fine = Mesh(mesh.devices.reshape(tuple(sizes.values())), tuple(sizes))
    grid = ("x", "h", "p", "w", "q", "c")
    specs = (P(grid, None, None), P(grid, None, None))
    return jax.shard_map(
        step, mesh=fine, in_specs=specs, out_specs=P(grid, "l", None), check_vma=False
    )
```

```python
import jax
import jax.numpy as jnp
from jax import lax
from jax.experimental import pallas as pl
from jax.experimental.pallas import tpu as pltpu
from jax.sharding import Mesh, PartitionSpec as P


SIZES = {"x": 4, "h": 2, "p": 2, "w": 4, "q": 2, "c": 2, "l": 2}
SMEM = pl.BlockSpec(memory_space=pltpu.SMEM)
VMEM = pl.BlockSpec(memory_space=pltpu.VMEM)
ANY = pl.BlockSpec(memory_space=pl.ANY)


def call(kernel, shape, dtype, specs, flops=0):
    size = 2
    for extent in shape:
        size *= extent
    return pl.pallas_call(
        kernel,
        out_shape=jax.ShapeDtypeStruct(shape, dtype),
        in_specs=specs,
        out_specs=VMEM,
        compiler_params=pltpu.CompilerParams(vmem_limit_bytes=16 << 20),
        cost_estimate=pl.CostEstimate(
            flops=flops, bytes_accessed=2 * size, transcendentals=0
        ),
    )


def exchange(blocks, axis):
    return lax.all_to_all(blocks, axis, 0, 0, tiled=True)


def swap(tile, axis):
    return lax.ppermute(tile, axis, ((0, 1), (1, 0)))


def total(blocks):
    return jnp.sum(blocks.astype(jnp.float32), axis=0)


def masked(tile, pattern):
    width, blocks = tile.shape[0], pattern.shape[0]
    span = width // blocks
    mask = jnp.broadcast_to(pattern[:, None, :, None], (blocks, span, blocks, span))
    return tile * mask.reshape(width, width).astype(tile.dtype)


def send_kernel(layer_ref, tile_ref, pattern_ref, out_ref, rows_ref, kept_ref, sems):
    share, width = out_ref.shape[1:]
    blocks = pattern_ref.shape[1]
    height = 4 * share
    small = share // 2
    span = width // blocks
    start = pl.multiple_of(layer_ref[0] * height, height)
    rows = pltpu.make_async_copy(tile_ref.at[0, pl.ds(start, height)], rows_ref, sems.at[0])
    kept = pltpu.make_async_copy(pattern_ref, kept_ref, sems.at[1])
    rows.start()
    kept.start()
    number = lax.broadcasted_iota(jnp.int32, (blocks, width), 0)
    place = lax.broadcasted_iota(jnp.int32, (blocks, width), 1)
    inside = (place >= number * span) & (place < number * span + span)
    kept.wait()
    wide = jnp.dot(
        kept_ref[0].astype(jnp.float32),
        inside.astype(jnp.float32),
        preferred_element_type=jnp.float32,
    )
    tall = lax.broadcasted_iota(jnp.int32, (height, blocks), 0) + start
    line = lax.broadcasted_iota(jnp.int32, (height, blocks), 1)
    chosen = (tall >= line * span) & (tall < line * span + span)
    mask = jnp.dot(chosen.astype(jnp.float32), wide, preferred_element_type=jnp.float32)
    rows.wait()
    piece = (rows_ref[...].astype(jnp.float32) * mask).astype(out_ref.dtype)
    for k in range(out_ref.shape[0]):
        p, c = k // 2 % 2, k % 2
        for q in range(2):
            part = (4 * p + 2 * q + c) * small
            out_ref[k, q * small : (q + 1) * small] = piece[part : part + small]


def rows_kernel(core_ref, parts_ref, out_ref):
    count, share, width = parts_ref.shape
    small = share // 2
    for k in range(count // 2):
        for side in range(2):
            columns = pl.ds(side * width, width)
            piece = parts_ref[2 * k + lax.bitwise_xor(core_ref[0], side)]
            for q in range(2):
                rows = pl.ds((q * (count // 2) + k) * small, small)
                for far in range(out_ref.shape[0]):
                    out_ref[far, rows, columns] = piece[q * small : (q + 1) * small]


def sum_kernel(parts_ref, out_ref):
    value = parts_ref[0].astype(jnp.float32)
    for k in range(1, parts_ref.shape[0]):
        value += parts_ref[k].astype(jnp.float32)
    for k in range(out_ref.shape[0]):
        out_ref[k] = value.astype(out_ref.dtype)


def first_kernel(rows_ref, a_ref, b_ref, c_ref, d_ref, out_ref):
    width = a_ref.shape[0]
    turned = (((1,), (1,)), ((), ()))
    left, right = rows_ref[:, :width], rows_ref[:, width:]
    for k, (one, two) in enumerate(((a_ref, b_ref), (c_ref, d_ref))):
        part = lax.dot_general(left, one[...], turned, preferred_element_type=jnp.float32)
        part += lax.dot_general(right, two[...], turned, preferred_element_type=jnp.float32)
        out_ref[:, k] = part.astype(out_ref.dtype).reshape(out_ref.shape[0], -1, width)


def second_kernel(place_ref, left_ref, *refs):
    tiles, lower, out_ref = refs[:4], refs[4:8], refs[8]
    width = tiles[0].shape[0]
    left = left_ref[:, 0].reshape(-1, width)
    right = left_ref[:, 1].reshape(-1, width)
    for k in range(4):
        part = jnp.dot(left, tiles[k][...], preferred_element_type=jnp.float32)
        part += jnp.dot(right, lower[k][...], preferred_element_type=jnp.float32)
        part = part.astype(out_ref.dtype).reshape(-1, out_ref.shape[2], width)
        out_ref[:, lax.bitwise_xor(place_ref[0], k)] = part


def step(x_tiles, pattern):
    half = jnp.bfloat16
    width = x_tiles.shape[1]
    share = width // 32
    nx, nw = lax.axis_size("x"), lax.axis_size("w")
    core = lax.axis_index("c").reshape(1)
    layer = lax.axis_index("l").reshape(1)
    height = 4 * nx * share
    flops = 8 * height * width * width

    parts = pl.pallas_call(
        send_kernel,
        out_shape=jax.ShapeDtypeStruct((8, share, width), half),
        in_specs=[SMEM, ANY, ANY],
        out_specs=VMEM,
        scratch_shapes=(
            pltpu.VMEM((4 * share, width), half),
            pltpu.VMEM(pattern.shape, jnp.int32),
            pltpu.SemaphoreType.DMA((2,)),
        ),
        name="send",
    )(layer, x_tiles, pattern)
    parts = exchange(parts, ("h", "p", "c"))
    rows = call(rows_kernel, (nx, 4 * share, 2 * width), half, [SMEM, VMEM])
    rows = exchange(rows(core, parts), "x").reshape(height, 2 * width)

    tile = masked(x_tiles[0], pattern[0])
    own = lax.dynamic_slice_in_dim(tile, layer[0] * 4 * share, 4 * share, 0)
    below = swap(tile, "p")
    along = swap(tile, "q")
    corner = swap(along, "p")
    tiles = [tile, swap(tile, "c"), along, swap(along, "c")]
    lower = [below, swap(below, "c"), corner, swap(corner, "c")]

    shape = (2 * nw, 2, height // (2 * nw), width)
    partial = call(first_kernel, shape, half, [VMEM] * 5, flops)
    partial = partial(rows, tiles[0], tiles[1], lower[0], lower[1])
    partial = exchange(partial.reshape(2 * nw, -1, width), ("w", "q"))
    squared = call(sum_kernel, (nw,) + partial.shape[1:], half, [VMEM])(partial)
    squared = exchange(squared, "w").reshape((nw,) + shape[1:])
    place = 2 * lax.axis_index("q") + lax.axis_index("c")
    shape = (4 * nx, 4, share // 2, width)
    parts = call(second_kernel, shape, half, [SMEM] + [VMEM] * 9, flops)
    parts = parts(place.reshape(1), squared, *tiles, *lower)
    parts = parts.reshape(16 * nx, share // 2, width)
    parts = exchange(parts, ("x", "h", "p", "q", "c"))
    cubed = total(parts.reshape(2 * nx, 4 * share, width))
    signed = 1.5 * own.astype(jnp.float32) - 0.5 * cubed
    return signed.astype(half)[None]


def solution(mesh, sizes=SIZES):
    fine = Mesh(mesh.devices.reshape(tuple(sizes.values())), tuple(sizes))
    grid = ("x", "h", "p", "w", "q", "c")
    specs = (P(grid, None, None), P(grid, None, None))
    return jax.shard_map(
        step, mesh=fine, in_specs=specs, out_specs=P(grid, "l", None), check_vma=False
    )
```

```python
import jax
import jax.numpy as jnp
from jax import lax
from jax.experimental import pallas as pl
from jax.experimental.pallas import tpu as pltpu
from jax.sharding import Mesh, PartitionSpec as P


SIZES = {"x": 4, "h": 2, "p": 2, "z": 8, "c": 2, "l": 2}
SMEM = pl.BlockSpec(memory_space=pltpu.SMEM)
VMEM = pl.BlockSpec(memory_space=pltpu.VMEM)
ANY = pl.BlockSpec(memory_space=pl.ANY)


def call(kernel, shape, dtype, specs, flops=0):
    size = 2
    for extent in shape:
        size *= extent
    return pl.pallas_call(
        kernel,
        out_shape=jax.ShapeDtypeStruct(shape, dtype),
        in_specs=specs,
        out_specs=VMEM,
        compiler_params=pltpu.CompilerParams(vmem_limit_bytes=16 << 20),
        cost_estimate=pl.CostEstimate(
            flops=flops, bytes_accessed=2 * size, transcendentals=0
        ),
    )


def exchange(blocks, axis):
    return lax.all_to_all(blocks, axis, 0, 0, tiled=True)


def swap(tile, axis):
    return lax.ppermute(tile, axis, ((0, 1), (1, 0)))


def total(blocks):
    return jnp.sum(blocks.astype(jnp.float32), axis=0)


def masked(tile, pattern):
    width, blocks = tile.shape[0], pattern.shape[0]
    span = width // blocks
    mask = jnp.broadcast_to(pattern[:, None, :, None], (blocks, span, blocks, span))
    return tile * mask.reshape(width, width).astype(tile.dtype)


def send_kernel(layer_ref, tile_ref, pattern_ref, out_ref, rows_ref, kept_ref, sems):
    share, width = out_ref.shape[1:]
    blocks = pattern_ref.shape[1]
    height = 4 * share
    span = width // blocks
    start = pl.multiple_of(layer_ref[0] * height, height)
    rows = pltpu.make_async_copy(tile_ref.at[0, pl.ds(start, height)], rows_ref, sems.at[0])
    kept = pltpu.make_async_copy(pattern_ref, kept_ref, sems.at[1])
    rows.start()
    kept.start()
    number = lax.broadcasted_iota(jnp.int32, (blocks, width), 0)
    place = lax.broadcasted_iota(jnp.int32, (blocks, width), 1)
    inside = (place >= number * span) & (place < number * span + span)
    kept.wait()
    wide = jnp.dot(
        kept_ref[0].astype(jnp.float32),
        inside.astype(jnp.float32),
        preferred_element_type=jnp.float32,
    )
    tall = lax.broadcasted_iota(jnp.int32, (height, blocks), 0) + start
    line = lax.broadcasted_iota(jnp.int32, (height, blocks), 1)
    chosen = (tall >= line * span) & (tall < line * span + span)
    mask = jnp.dot(chosen.astype(jnp.float32), wide, preferred_element_type=jnp.float32)
    rows.wait()
    piece = (rows_ref[...].astype(jnp.float32) * mask).astype(out_ref.dtype)
    for k in range(out_ref.shape[0]):
        part = k % 4 * share
        out_ref[k] = piece[part : part + share]


def rows_kernel(core_ref, parts_ref, out_ref):
    share, width = parts_ref.shape[1:]
    for k in range(parts_ref.shape[0] // 2):
        for side in range(2):
            piece = parts_ref[2 * k + lax.bitwise_xor(core_ref[0], side)]
            for far in range(out_ref.shape[0]):
                rows, columns = pl.ds(k * share, share), pl.ds(side * width, width)
                out_ref[far, rows, columns] = piece


def first_kernel(rows_ref, a_ref, b_ref, c_ref, d_ref, out_ref):
    width = a_ref.shape[0]
    turned = (((1,), (1,)), ((), ()))
    left, right = rows_ref[:, :width], rows_ref[:, width:]
    for k, (one, two) in enumerate(((a_ref, b_ref), (c_ref, d_ref))):
        part = lax.dot_general(left, one[...], turned, preferred_element_type=jnp.float32)
        part += lax.dot_general(right, two[...], turned, preferred_element_type=jnp.float32)
        out_ref[:, k] = part.astype(out_ref.dtype).reshape(out_ref.shape[0], -1, width)


def second_kernel(core_ref, left_ref, a_ref, b_ref, c_ref, d_ref, out_ref):
    width = a_ref.shape[0]
    left = left_ref[:, 0].reshape(-1, width)
    right = left_ref[:, 1].reshape(-1, width)
    for k, (one, two) in enumerate(((a_ref, c_ref), (b_ref, d_ref))):
        part = jnp.dot(left, one[...], preferred_element_type=jnp.float32)
        part += jnp.dot(right, two[...], preferred_element_type=jnp.float32)
        part = part.astype(out_ref.dtype).reshape(out_ref.shape[0], -1, width)
        out_ref[:, lax.bitwise_xor(core_ref[0], k)] = part


def sum_kernel(parts_ref, out_ref):
    share = out_ref.shape[1]
    value = parts_ref[0].astype(jnp.float32)
    for k in range(1, parts_ref.shape[0]):
        value += parts_ref[k].astype(jnp.float32)
    value = value.astype(out_ref.dtype)
    for k in range(out_ref.shape[0]):
        out_ref[k] = value[k % 2, k // 2 * share : (k // 2 + 1) * share]


def step(x_tiles, pattern):
    half = jnp.bfloat16
    width = x_tiles.shape[1]
    share = width // 32
    nx, nz = lax.axis_size("x"), lax.axis_size("z")
    core = lax.axis_index("c").reshape(1)
    layer = lax.axis_index("l").reshape(1)
    height = 4 * nx * share
    flops = 8 * height * width * width

    parts = pl.pallas_call(
        send_kernel,
        out_shape=jax.ShapeDtypeStruct((8, share, width), half),
        in_specs=[SMEM, ANY, ANY],
        out_specs=VMEM,
        scratch_shapes=(
            pltpu.VMEM((4 * share, width), half),
            pltpu.VMEM(pattern.shape, jnp.int32),
            pltpu.SemaphoreType.DMA((2,)),
        ),
        name="send",
    )(layer, x_tiles, pattern)
    index = lax.axis_index("l").astype(jnp.uint32) * (4 * share)
    parts, index = lax.optimization_barrier((parts, index))
    parts = exchange(parts, ("h", "p", "c"))
    rows = call(rows_kernel, (nx, 4 * share, 2 * width), half, [SMEM, VMEM])
    rows = exchange(rows(core, parts), "x").reshape(height, 2 * width)

    tile = masked(x_tiles[0], pattern[0])
    own = lax.dynamic_slice(tile, (index, jnp.uint32(0)), (4 * share, width))
    below = swap(tile, "p")
    tiles = [tile, swap(tile, "c"), below, swap(below, "c")]

    shape = (nz, 2, height // nz, width)
    partial = call(first_kernel, shape, half, [VMEM] * 5, flops)(rows, *tiles)
    partial = partial.reshape(nz, -1, width)
    squared = total(exchange(partial, "z")).astype(half)
    squared = jnp.broadcast_to(squared[None], (nz,) + squared.shape)
    squared = exchange(squared, "z").reshape(shape)
    shape = (nx, 2, 4 * share, width)
    parts = call(second_kernel, shape, half, [SMEM] + [VMEM] * 5, flops)
    parts = parts(core, squared, *tiles).reshape(nx, 8 * share, width)
    parts = exchange(parts, "x").reshape(shape)
    parts = call(sum_kernel, (8, share, width), half, [VMEM])(parts)
    parts = exchange(parts, ("h", "p", "c"))
    cubed = total(parts.reshape(2, 4 * share, width))
    signed = 1.5 * own.astype(jnp.float32) - 0.5 * cubed
    return signed.astype(half)[None]


def solution(mesh, sizes=SIZES):
    fine = Mesh(mesh.devices.reshape(tuple(sizes.values())), tuple(sizes))
    grid = ("x", "h", "p", "z", "c")
    specs = (P(grid, None, None), P(grid, None, None))
    return jax.shard_map(
        step, mesh=fine, in_specs=specs, out_specs=P(grid, "l", None), check_vma=False
    )
```

```python
import jax
import jax.numpy as jnp
from jax import lax
from jax.experimental import pallas as pl
from jax.experimental.pallas import tpu as pltpu
from jax.sharding import Mesh, PartitionSpec as P


SIZES = {"x": 4, "h": 2, "p": 2, "z": 8, "c": 2, "l": 2}
SMEM = pl.BlockSpec(memory_space=pltpu.SMEM)
VMEM = pl.BlockSpec(memory_space=pltpu.VMEM)
ANY = pl.BlockSpec(memory_space=pl.ANY)


def call(kernel, shape, dtype, specs, flops=0):
    size = 2
    for extent in shape:
        size *= extent
    return pl.pallas_call(
        kernel,
        out_shape=jax.ShapeDtypeStruct(shape, dtype),
        in_specs=specs,
        out_specs=VMEM,
        compiler_params=pltpu.CompilerParams(vmem_limit_bytes=16 << 20),
        cost_estimate=pl.CostEstimate(
            flops=flops, bytes_accessed=2 * size, transcendentals=0
        ),
    )


def exchange(blocks, axis):
    return lax.all_to_all(blocks, axis, 0, 0, tiled=True)


def swap(tile, axis):
    return lax.ppermute(tile, axis, ((0, 1), (1, 0)))


def total(blocks):
    return jnp.sum(blocks.astype(jnp.float32), axis=0)


def masked(tile, pattern):
    width, blocks = tile.shape[0], pattern.shape[0]
    span = width // blocks
    mask = jnp.broadcast_to(pattern[:, None, :, None], (blocks, span, blocks, span))
    return tile * mask.reshape(width, width).astype(tile.dtype)


def send_kernel(layer_ref, tile_ref, pattern_ref, out_ref, rows_ref, kept_ref, sems):
    share, width = out_ref.shape[1:]
    blocks = pattern_ref.shape[1]
    height = 4 * share
    span = width // blocks
    start = pl.multiple_of(layer_ref[0] * height, height)
    rows = pltpu.make_async_copy(tile_ref.at[0, pl.ds(start, height)], rows_ref, sems.at[0])
    kept = pltpu.make_async_copy(pattern_ref, kept_ref, sems.at[1])
    rows.start()
    kept.start()
    number = lax.broadcasted_iota(jnp.int32, (blocks, width), 0)
    place = lax.broadcasted_iota(jnp.int32, (blocks, width), 1)
    inside = (place >= number * span) & (place < number * span + span)
    kept.wait()
    wide = jnp.dot(
        kept_ref[0].astype(jnp.float32),
        inside.astype(jnp.float32),
        preferred_element_type=jnp.float32,
    )
    tall = lax.broadcasted_iota(jnp.int32, (height, blocks), 0) + start
    line = lax.broadcasted_iota(jnp.int32, (height, blocks), 1)
    chosen = (tall >= line * span) & (tall < line * span + span)
    mask = jnp.dot(chosen.astype(jnp.float32), wide, preferred_element_type=jnp.float32)
    rows.wait()
    piece = (rows_ref[...].astype(jnp.float32) * mask).astype(out_ref.dtype)
    for k in range(out_ref.shape[0]):
        part = k % 4 * share
        out_ref[k] = piece[part : part + share]


def rows_kernel(core_ref, parts_ref, out_ref):
    share, _ = parts_ref.shape[1:]
    for k in range(parts_ref.shape[0] // 2):
        for side in range(2):
            piece = parts_ref[2 * k + lax.bitwise_xor(core_ref[0], side)]
            for far in range(out_ref.shape[0]):
                out_ref[far, side, pl.ds(k * share, share)] = piece


def first_kernel(rows_ref, a_ref, b_ref, c_ref, d_ref, out_ref):
    width = a_ref.shape[0]
    turned = (((1,), (1,)), ((), ()))
    left = rows_ref[:, 0].reshape(-1, width)
    right = rows_ref[:, 1].reshape(-1, width)
    for k, (one, two) in enumerate(((a_ref, b_ref), (c_ref, d_ref))):
        part = lax.dot_general(left, one[...], turned, preferred_element_type=jnp.float32)
        part += lax.dot_general(right, two[...], turned, preferred_element_type=jnp.float32)
        out_ref[:, k] = part.astype(out_ref.dtype).reshape(out_ref.shape[0], -1, width)


def second_kernel(core_ref, left_ref, a_ref, b_ref, c_ref, d_ref, out_ref):
    width = a_ref.shape[0]
    left = left_ref[:, 0].reshape(-1, width)
    right = left_ref[:, 1].reshape(-1, width)
    for k, (one, two) in enumerate(((a_ref, c_ref), (b_ref, d_ref))):
        part = jnp.dot(left, one[...], preferred_element_type=jnp.float32)
        part += jnp.dot(right, two[...], preferred_element_type=jnp.float32)
        part = part.astype(out_ref.dtype).reshape(out_ref.shape[0], -1, width)
        out_ref[:, lax.bitwise_xor(core_ref[0], k)] = part


def sum_kernel(parts_ref, out_ref):
    share = out_ref.shape[1]
    value = parts_ref[0].astype(jnp.float32)
    for k in range(1, parts_ref.shape[0]):
        value += parts_ref[k].astype(jnp.float32)
    value = value.astype(out_ref.dtype)
    for k in range(out_ref.shape[0]):
        out_ref[k] = value[k % 2, k // 2 * share : (k // 2 + 1) * share]


def step(x_tiles, pattern):
    half = jnp.bfloat16
    width = x_tiles.shape[1]
    share = width // 32
    nx, nz = lax.axis_size("x"), lax.axis_size("z")
    core = lax.axis_index("c").reshape(1)
    layer = lax.axis_index("l").reshape(1)
    height = 4 * nx * share
    flops = 8 * height * width * width

    parts = pl.pallas_call(
        send_kernel,
        out_shape=jax.ShapeDtypeStruct((8, share, width), half),
        in_specs=[SMEM, ANY, ANY],
        out_specs=VMEM,
        scratch_shapes=(
            pltpu.VMEM((4 * share, width), half),
            pltpu.VMEM(pattern.shape, jnp.int32),
            pltpu.SemaphoreType.DMA((2,)),
        ),
        name="send",
    )(layer, x_tiles, pattern)
    index = lax.axis_index("l").astype(jnp.uint32) * (4 * share)
    parts, index = lax.optimization_barrier((parts, index))
    parts = exchange(parts, ("h", "p", "c"))
    shape = (nx, 2, 4 * share, width)
    rows = call(rows_kernel, shape, half, [SMEM, VMEM])(core, parts)
    rows = exchange(rows.reshape(nx, 8 * share, width), "x").reshape(shape)

    tile = masked(x_tiles[0], pattern[0])
    own = lax.dynamic_slice(tile, (index, jnp.uint32(0)), (4 * share, width))
    below = swap(tile, "p")
    tiles = [tile, swap(tile, "c"), below, swap(below, "c")]

    shape = (nz, 2, height // nz, width)
    partial = call(first_kernel, shape, half, [VMEM] * 5, flops)(rows, *tiles)
    partial = partial.reshape(nz, -1, width)
    squared = total(exchange(partial, "z")).astype(half)
    squared = jnp.broadcast_to(squared[None], (nz,) + squared.shape)
    squared = exchange(squared, "z").reshape(shape)
    shape = (nx, 2, 4 * share, width)
    parts = call(second_kernel, shape, half, [SMEM] + [VMEM] * 5, flops)
    parts = parts(core, squared, *tiles).reshape(nx, 8 * share, width)
    parts = exchange(parts, "x").reshape(shape)
    parts = call(sum_kernel, (8, share, width), half, [VMEM])(parts)
    parts = exchange(parts, ("h", "p", "c"))
    cubed = total(parts.reshape(2, 4 * share, width))
    signed = 1.5 * own.astype(jnp.float32) - 0.5 * cubed
    return signed.astype(half)[None]


def solution(mesh, sizes=SIZES):
    fine = Mesh(mesh.devices.reshape(tuple(sizes.values())), tuple(sizes))
    grid = ("x", "h", "p", "z", "c")
    specs = (P(grid, None, None), P(grid, None, None))
    return jax.shard_map(
        step, mesh=fine, in_specs=specs, out_specs=P(grid, "l", None), check_vma=False
    )
```
